32 devices in a mesh: grp: 2 (over y), node: 4 (over z), rank: 4 (over x, core).
Axes of the slice: x: 2, y: 2, z: 4, core: 2. Of those that a mesh axis runs over, the one named last changes fastest.
Arguments:
- tokens: bfloat16 [1024, 2048], P(('grp', 'node', 'rank')), parts along dimension 0, may hold values from -6 to 6
- expert_ids: int32 [1024, 10], P(('grp', 'node', 'rank')), parts along dimension 0, may hold values from 0 to 31, all different within a row; in each aligned block of 32 rows (0 to 31, 32 to 63, ...) at most 15 rows name the same one
- combine_weights: int32 [1024, 10], P(('grp', 'node', 'rank')), parts along dimension 0, may hold values from 16384 to 65535
- slot_plan: int32 [32], replicated, may hold values from 0 to 31, each once
- w_gate: bfloat16 [32, 2048, 512], P(('node', 'rank')), may hold values from -0.125 to 0.125
- w_up: bfloat16 [32, 2048, 512], P(('node', 'rank')), may hold values from -0.125 to 0.125
- w_down: bfloat16 [32, 512, 2048], P(('node', 'rank')), may hold values from -0.25 to 0.25
Outputs:
- mixed: bfloat16 [1024, 2048], P(('grp', 'node', 'rank')), parts along dimension 0
The draws below stay inside these ranges and needn't reach their ends.
There are 2 independent parts, one for each index of `grp`. The reference program is written for one: setup_inputs(seed, part) draws one part's arguments, and reference() takes and returns one part's arrays. A program takes and returns all parts, laid end to end along the dimension named above; an argument that names none is the same for every part. Nothing has to cross between parts.
Inputs may be any that keep to these rules, and one draw needn't show every extreme that they name: `expert_ids`: each row names 10 different experts; among the rows of one device no expert is named more than 15 times, and in every draw some expert reaches 15. `slot_plan`: each slot once.
All inputs are finite; a program needn't handle non-finite values.
Results may differ from the reference program's by a relative error of at most 0.0058.
Values may be sent and summed in bfloat16 or wider, within the bound.
A program may use at most 64 MiB of HBM per device.

```python
import math
import jax
import jax.numpy as jnp
import numpy as np
from jax import lax

D = 2048
FF = 512
TOP = 10
TOK_DEV = 32
EXPERTS = 32
TOKENS = 512
CAP = 15
ROWS = 240


def touch_ends(drawn, stream_key, smallest, high):
    longest = drawn.shape.index(max(drawn.shape))
    spots = []
    for shift in (0, 1):
        where = [jax.random.randint(jax.random.fold_in(stream_key, axis), (), 0, length) for axis, length in enumerate(drawn.shape)]
        where[longest] = (where[longest] + shift) % drawn.shape[longest]
        spots.append(tuple(where))
    return drawn.at[spots[0]].set(smallest).at[spots[1]].set(high)


def levels(key, extent, shards, smallest, high):
    factor_of, own = 1.0, jax.random.fold_in(key, 6)
    for dim, parts in shards:
        heights = jnp.exp(jax.random.uniform(jax.random.fold_in(own, dim), (parts,), jnp.float32, smallest / len(shards), high / len(shards)))
        factor_of = factor_of * jnp.repeat(heights, extent[dim] // parts).reshape([-1 if axis == dim else 1 for axis in range(len(extent))])
    return factor_of


def routed_block(own_key, own, number, rows, count, top, bound, skew):
    ranking = jax.random.permutation(own_key, count)
    heavy_load, ordinary = shares(count, rows * top, bound, skew, True), shares(count, rows * top, bound, skew, False)
    places = jnp.arange(count)

    def named(tallies, rotation):
        used = int((tallies > 0).sum())
        fixed = max(1, used // 4)
        shifted = fixed + (places - fixed + rotation * (used - fixed)) % max(1, count - fixed)
        return jnp.zeros((count,), jnp.int32).at[ranking[jnp.where(places < fixed, places, shifted)]].set(jnp.asarray(tallies, jnp.int32))

    tallies = jnp.where(number % 4 == 0, named(heavy_load, number // 4), named(ordinary, number - number // 4 - 1))
    mixed = jax.random.permutation(jax.random.fold_in(own, 3), count)
    donor, receiver = mixed[0:count // 2 * 2:2], mixed[1:count // 2 * 2:2]
    slack = jnp.minimum(tallies[donor] - 1, bound - tallies[receiver]) // 2
    slack = jnp.where((donor == ranking[0]) | (receiver == ranking[0]) | (tallies[receiver] == 0), 0, jnp.maximum(slack, 0))
    shifted = jax.random.randint(jax.random.fold_in(own, 4), (count // 2,), 0, 1 << 20) % (slack + 1)
    tallies = tallies.at[donor].add(-shifted).at[receiver].add(shifted)
    labels = jnp.searchsorted(jnp.cumsum(tallies), jnp.arange(rows * top), side="right").astype(jnp.int32)
    grid = labels.reshape(top, rows).T
    grid = grid[jax.random.permutation(jax.random.fold_in(own, 1), rows)]
    rotation = jax.random.randint(jax.random.fold_in(own, 2), (rows, 1), 0, top)
    return jnp.take_along_axis(grid, (jnp.arange(top)[None, :] + rotation) % top, axis=1)


def shares(count, total, most, slope, full):
    weights = [(1 << 20) // math.isqrt(standing ** slope) + 1 for standing in range(1, count + 1)]
    largest = most if full else min(most, max(-(-total // count), total * weights[0] // sum(weights)))
    least = 1 if total - largest >= count - 1 else 0
    counts, rest = [largest] + [least] * (count - 1), total - largest - least * (count - 1)
    while rest > 0:
        movable = [i for i in range(1, count) if counts[i] < largest] or [i for i in range(1, count) if counts[i] < most]
        pool, remaining = sum([weights[i] for i in movable]), rest
        for i in movable:
            more = min(most - counts[i], max(1, remaining * weights[i] // pool), rest)
            counts[i] = counts[i] + more
            rest = rest - more
    return np.array(counts)


def normal_values(stream_key, extent, width, limit, split=(), kind=jnp.bfloat16):
    values = width * jax.random.normal(stream_key, extent, jnp.float32)
    if split:
        values = values * levels(stream_key, extent, split, -0.22, 0.18)
    return jnp.clip(values, -limit, limit).astype(kind)


def setup_inputs(seed: int = 0, part: int = 0) -> dict:
    streams_of = jax.random.split(jax.random.key(seed), 8)
    part_splits = jax.random.split(jax.random.fold_in(streams_of[7], part), 8)
    tokens = normal_values(part_splits[0], (TOKENS, D), 1.0, 6.0, ((0, 16),))
    expert_ids_keys = jax.random.split(jax.random.fold_in(part_splits[1], 1), TOKENS // TOK_DEV)
    expert_ids_turns = jax.random.permutation(jax.random.fold_in(part_splits[1], 3), TOKENS // TOK_DEV)
    expert_ids = jax.vmap(lambda own, number: routed_block(jax.random.fold_in(part_splits[1], 2), own, number, TOK_DEV, EXPERTS, TOP, CAP, 2))(expert_ids_keys, expert_ids_turns).reshape((TOKENS, TOP))
    combine_weights = touch_ends(jax.random.randint(part_splits[2], (TOKENS, TOP), 16384, 65536), jax.random.fold_in(part_splits[2], 1), 16384, 65535).astype(jnp.int32)
    slot_plan = jax.random.permutation(streams_of[3], EXPERTS).astype(jnp.int32)
    w_gate = normal_values(streams_of[4], (EXPERTS, D, FF), D ** -0.5, 0.125, ((0, 16),))
    w_up = normal_values(streams_of[5], (EXPERTS, D, FF), D ** -0.5, 0.125, ((0, 16),))
    w_down = normal_values(streams_of[6], (EXPERTS, FF, D), FF ** -0.5, 0.25, ((0, 16),))
    return dict(tokens=tokens, expert_ids=expert_ids, combine_weights=combine_weights, slot_plan=slot_plan, w_gate=w_gate, w_up=w_up, w_down=w_down)


def reference(tokens, expert_ids, combine_weights, slot_plan, w_gate, w_up, w_down):
    flat_ids = expert_ids.reshape(-1)
    flat_weights = combine_weights.reshape(-1).astype(jnp.float32) / 65536.0
    lanes = jnp.arange(ROWS, dtype=jnp.int32)

    def one_expert(total, expert):
        slot = slot_plan[expert]
        chosen = flat_ids == expert
        count = jnp.sum(chosen.astype(jnp.int32))
        picked = jnp.nonzero(chosen, size=ROWS, fill_value=0)[0].astype(jnp.int32)
        token_rows = (picked // TOP).astype(jnp.int32)
        rows = tokens[token_rows]
        gate = jnp.dot(rows, w_gate[slot], preferred_element_type=jnp.float32)
        up = jnp.dot(rows, w_up[slot], preferred_element_type=jnp.float32)
        hidden = (jax.nn.silu(gate) * up).astype(jnp.bfloat16)
        result = jnp.dot(hidden, w_down[slot], preferred_element_type=jnp.float32).astype(jnp.bfloat16)
        scale = jnp.where(lanes < count, flat_weights[picked], 0.0).astype(jnp.float32)
        total = total.at[token_rows].add(result.astype(jnp.float32) * scale[:, None])
        return total, None

    start = jnp.zeros((TOKENS, D), jnp.float32)
    total, _ = lax.scan(one_expert, start, jnp.arange(EXPERTS, dtype=jnp.int32))
    return total.astype(jnp.bfloat16)
```

```python
import functools
import jax
import jax.numpy as jnp
from jax import lax
from jax.experimental import pallas as pl
from jax.experimental.pallas import tpu as pltpu
from jax.sharding import PartitionSpec as P

CORES = 2
CHUNKS = 4
MESH = pl.DeviceIdType.MESH
UP, DOWN, CROSS, TWIN, RELAY = range(5)


def sparse_local(tokens, expert_ids, combine_weights, slot_plan, w_gate, w_up, w_down):
    n_node = lax.axis_size("node")
    n_rank = lax.axis_size("rank")
    n_dev = n_node * n_rank
    exp_dev = w_gate.shape[0]
    slots = n_dev * exp_dev
    tok_rows, top = expert_ids.shape
    width = tokens.shape[1]
    capacity = max(2, (3 * tok_rows * top + 2 * slots - 1) // (2 * slots))
    flat_ids = expert_ids.reshape(-1)
    onehot = (flat_ids[:, None] == jnp.arange(slots, dtype=jnp.int32)[None, :]).astype(jnp.int32)
    slot_of = jnp.sum(onehot * slot_plan[None, :], axis=1)
    earlier = jnp.cumsum(onehot, axis=0) - onehot
    position = jnp.sum(earlier * onehot, axis=1)
    target = slot_of * capacity + position
    repeated = jnp.repeat(tokens, top, axis=0)
    outgoing = jnp.zeros((slots * capacity, width), jnp.bfloat16).at[target].set(repeated)
    flat_out = outgoing.reshape(n_dev, exp_dev * capacity, width)
    arrived = lax.all_to_all(flat_out, ("node", "rank"), split_axis=0, concat_axis=0, tiled=True)
    arrived = arrived.reshape(n_dev, exp_dev, capacity, width)
    gate = jnp.einsum("secd,edf->secf", arrived, w_gate, preferred_element_type=jnp.float32)
    up = jnp.einsum("secd,edf->secf", arrived, w_up, preferred_element_type=jnp.float32)
    hidden = (jax.nn.silu(gate) * up).astype(jnp.bfloat16)
    result = jnp.einsum(
        "secf,efd->secd", hidden, w_down, preferred_element_type=jnp.float32
    ).astype(jnp.bfloat16)
    flat_back = result.reshape(n_dev, exp_dev * capacity, width)
    returned = lax.all_to_all(flat_back, ("node", "rank"), split_axis=0, concat_axis=0, tiled=True)
    returned = returned.reshape(slots * capacity, width)
    picked = returned[target].reshape(tok_rows, top, width)
    scales = combine_weights.astype(jnp.float32) / 65536.0
    mixed = jnp.sum(picked.astype(jnp.float32) * scales[:, :, None], axis=1)
    return mixed.astype(jnp.bfloat16)


def kernel(
    nz, experts, tok_hbm, ids_ref, wts_ref, plan_ref, wg_hbm, wu_hbm, wd_hbm, out_ref,
    *scratch,
):
    bufs = scratch[:CHUNKS]
    (wgu, wdn, acc, hid, s1, r1, k1, s2, r2, az, su, ru, sd, rd,
     own_sem, wgu_sem, wd_sem, send_sem, recv_sem,
     s1_sem, r1_sem, s2_sem, r2_sem, su_sem, ru_sem, sd_sem, rd_sem) = scratch[CHUNKS:]
    z = lax.axis_index("node")
    rank = lax.axis_index("rank")
    x, c = rank // CORES, rank % CORES
    rows, width = tok_hbm.shape
    cols = width // CHUNKS
    exp_dev, _, ff = wg_hbm.shape
    col_rows = nz * rows
    half = 2 * nz
    total_rows = 2 * half * rows
    mine = c * half + x * nz
    other = c * half + (1 - x) * nz
    above, below = {"node": z + 1}, {"node": z - 1}
    across = {"rank": (1 - x) * CORES + c}
    twin = {"rank": x * CORES + (1 - c)}

    own = [
        pltpu.make_async_copy(
            tok_hbm.at[:, pl.ds(j * cols, cols)],
            bufs[j].at[mine + z, :, pl.ds(0, cols)],
            own_sem.at[j],
        )
        for j in range(CHUNKS)
    ]
    for copy in own:
        copy.start()

    barrier = pltpu.get_barrier_semaphore()

    def greet(device):
        pl.semaphore_signal(barrier, inc=1, device_id=device, device_id_type=MESH)

    greet(across)
    greet(twin)
    pl.when(z < nz - 1)(lambda: greet(above))
    pl.when(z > 0)(lambda: greet(below))

    gu_copies = []
    for j in range(CHUNKS):
        piece = []
        for e in range(exp_dev):
            for g, src in enumerate((wg_hbm, wu_hbm)):
                i = e * 2 + g
                piece.append(pltpu.make_async_copy(
                    src.at[e, pl.ds(j * cols, cols), :],
                    wgu.at[i, pl.ds(j * cols, cols), :],
                    wgu_sem.at[j, i],
                ))
        gu_copies.append(piece)
    d_copies = [
        pltpu.make_async_copy(wd_hbm.at[e], wdn.at[pl.ds(e * ff, ff), :], wd_sem.at[e])
        for e in range(exp_dev)
    ]
    for piece in gu_copies:
        for copy in piece:
            copy.start()
    for copy in d_copies:
        copy.start()

    mix_w = bufs[0].shape[2] - cols
    lane = lax.broadcasted_iota(jnp.int32, (rows, mix_w), 1)
    low = lane >= experts
    expert = jnp.where(low, lane - experts, lane)
    ids, wts = ids_ref[...], wts_ref[...]
    dense = jnp.zeros((rows, mix_w), jnp.int32)
    for k in range(ids.shape[1]):
        dense += jnp.where(ids[:, k:k + 1] == expert, wts[:, k:k + 1], 0)
    parts = jnp.where(low, dense & 255, dense >> 8)
    bufs[0][mine + z, :, cols:] = parts.astype(jnp.float32).astype(jnp.bfloat16)

    peers = 2 + (z < nz - 1).astype(jnp.int32) + (z > 0).astype(jnp.int32)
    pl.semaphore_wait(barrier, peers)

    def block_copy(j, slot, kind, row, device):
        return pltpu.make_async_remote_copy(
            src_ref=bufs[j].at[slot],
            dst_ref=bufs[j].at[slot],
            send_sem=send_sem.at[j, kind, row],
            recv_sem=recv_sem.at[j, slot],
            device_id=device,
            device_id_type=MESH,
        )

    def arrived(j, slot):
        block_copy(j, slot, RELAY, 0, twin).wait_recv()

    def spread(j, src, go_up, go_down):
        if go_up:
            pl.when(z < nz - 1)(lambda: block_copy(j, mine + src, UP, src, above).start())
        if go_down:
            pl.when(z > 0)(lambda: block_copy(j, mine + src, DOWN, src, below).start())
        block_copy(j, mine + src, CROSS, src, across).start()
        block_copy(j, mine + src, TWIN, src, twin).start()

    def relay(j, src):
        arrived(j, other + src)
        block_copy(j, other + src, RELAY, src, twin).start()

    def gather_step(j, dist):
        if dist == 0:
            own[j].wait()
            spread(j, z, True, True)
        elif dist < nz:
            @pl.when(z - dist >= 0)
            def _():
                arrived(j, mine + z - dist)
                spread(j, z - dist, True, False)

            @pl.when(z + dist <= nz - 1)
            def _():
                arrived(j, mine + z + dist)
                spread(j, z + dist, False, True)
        if dist >= 1:
            if dist == 1:
                relay(j, z)
            else:
                pl.when(z - dist + 1 >= 0)(lambda: relay(j, z - dist + 1))
                pl.when(z + dist - 1 <= nz - 1)(lambda: relay(j, z + dist - 1))

    def project(j):
        for s in range(half):
            arrived(j, (1 - c) * half + s)
        for copy in gu_copies[j]:
            copy.wait()

        def one(i, carry):
            block = bufs[j][:, :, :cols].reshape(total_rows, cols)
            part = jnp.dot(
                block, wgu[i, pl.ds(j * cols, cols), :], preferred_element_type=jnp.float32
            )
            if j == 0:
                acc[i] = part
            else:
                acc[i] = acc[i] + part
            return carry

        lax.fori_loop(0, 2 * exp_dev, one, 0)

    for wave in range(CHUNKS + nz):
        for dist in range(nz + 1):
            j = wave - dist
            if 0 <= j < CHUNKS:
                gather_step(j, dist)
        if 0 <= wave - nz < CHUNKS:
            project(wave - nz)

    device = z * lax.axis_size("rank") + rank
    mixes = bufs[0][:, :, cols:].reshape(total_rows, mix_w).astype(jnp.float32)
    lane_row = lax.broadcasted_iota(jnp.int32, (1, mix_w), 1)
    unit = jnp.where(lane_row < experts, 256.0 / 65536.0, 1.0 / 65536.0)
    for e in range(exp_dev):
        pick = jnp.where(plan_ref[...] == device * exp_dev + e, unit, 0.0)
        scale = jnp.sum(mixes * pick, axis=1, keepdims=True)
        gate = acc[2 * e]
        value = gate / (1.0 + jnp.exp(-gate)) * acc[2 * e + 1]
        hid[:, e * ff:(e + 1) * ff] = (value * scale).astype(jnp.bfloat16)
    for copy in d_copies:
        copy.wait()

    half_rows = half * rows

    def push(src, dst, ssem, rsem, dev):
        return pltpu.make_async_remote_copy(
            src_ref=src, dst_ref=dst, send_sem=ssem, recv_sem=rsem,
            device_id=dev, device_id_type=MESH,
        )

    def twin_copy(j):
        return push(s1.at[j], r1.at[j], s1_sem.at[j], r1_sem.at[j], twin)

    def cross_copy(j):
        return push(s2.at[j], r2.at[j], s2_sem.at[j], r2_sem.at[j], across)

    def up_copy(j, t):
        return push(su.at[j, t], ru.at[j, t], su_sem.at[j, t], ru_sem.at[j, t], above)

    def down_copy(j, t):
        return push(sd.at[j, t], rd.at[j, t], sd_sem.at[j, t], rd_sem.at[j, t], below)

    def stage_down(j):
        w = wdn[:, j * cols:(j + 1) * cols]
        s1[j] = jnp.dot(
            hid[pl.ds((1 - c) * half_rows, half_rows), :], w, preferred_element_type=jnp.float32
        ).astype(jnp.bfloat16)
        twin_copy(j).start()
        k1[j] = jnp.dot(
            hid[pl.ds(c * half_rows, half_rows), :], w, preferred_element_type=jnp.float32
        )

    def stage_cross(j):
        twin_copy(j).wait_recv()
        away = pl.ds((1 - x) * col_rows, col_rows)
        s2[j] = (k1[j, away, :] + r1[j, away, :].astype(jnp.float32)).astype(jnp.bfloat16)
        cross_copy(j).start()

    def stage_column(j):
        cross_copy(j).wait_recv()
        near = pl.ds(x * col_rows, col_rows)
        total = k1[j, near, :] + r1[j, near, :].astype(jnp.float32) + r2[j].astype(jnp.float32)
        az[j] = total.reshape(nz, rows, cols)

    def stage_chain(j):
        for t in range(nz - 1, 0, -1):
            @pl.when(z == 0)
            def _():
                su[j, t] = az[j, t].astype(jnp.bfloat16)
                up_copy(j, t).start()

            @pl.when((z > 0) & (z < t))
            def _():
                up_copy(j, t).wait_recv()
                su[j, t] = (az[j, t] + ru[j, t].astype(jnp.float32)).astype(jnp.bfloat16)
                up_copy(j, t).start()
        for t in range(nz - 1):
            @pl.when(z == nz - 1)
            def _():
                sd[j, t] = az[j, t].astype(jnp.bfloat16)
                down_copy(j, t).start()

            @pl.when((z < nz - 1) & (z > t))
            def _():
                down_copy(j, t).wait_recv()
                sd[j, t] = (az[j, t] + rd[j, t].astype(jnp.float32)).astype(jnp.bfloat16)
                down_copy(j, t).start()

    def stage_final(j):
        @pl.when(z > 0)
        def _():
            up_copy(j, z).wait_recv()
            az[j, z] = az[j, z] + ru[j, z].astype(jnp.float32)

        @pl.when(z < nz - 1)
        def _():
            down_copy(j, z).wait_recv()
            az[j, z] = az[j, z] + rd[j, z].astype(jnp.float32)

        out_ref[:, j * cols:(j + 1) * cols] = az[j, z].astype(jnp.bfloat16)

    stages = (stage_down, stage_cross, stage_column, stage_chain, stage_final)
    for wave in range(CHUNKS + len(stages) - 1):
        for s, stage in enumerate(stages):
            if 0 <= wave - s < CHUNKS:
                stage(wave - s)

    for j in range(CHUNKS):
        for src in range(nz):
            pl.when((z < nz - 1) & (src <= z))(
                lambda: block_copy(j, mine + src, UP, src, above).wait_send())
            pl.when((z > 0) & (src >= z))(
                lambda: block_copy(j, mine + src, DOWN, src, below).wait_send())
            block_copy(j, mine + src, CROSS, src, across).wait_send()
            block_copy(j, mine + src, TWIN, src, twin).wait_send()
            block_copy(j, other + src, RELAY, src, twin).wait_send()
        twin_copy(j).wait_send()
        cross_copy(j).wait_send()
        for t in range(nz):
            pl.when(z < t)(lambda: up_copy(j, t).wait_send())
            pl.when(z > t)(lambda: down_copy(j, t).wait_send())


def dense_local(tokens, expert_ids, combine_weights, slot_plan, w_gate, w_up, w_down):
    nz = lax.axis_size("node")
    n_dev = nz * lax.axis_size("rank")
    rows, width = tokens.shape
    exp_dev, _, ff = w_gate.shape
    experts = slot_plan.shape[0]
    cols = width // CHUNKS
    mix_w = -(-2 * experts // 128) * 128
    plan = jnp.concatenate(
        [slot_plan, slot_plan, jnp.full((mix_w - 2 * experts,), -1, jnp.int32)]
    )[None, :]
    half = 2 * nz
    half_rows, col_rows = half * rows, nz * rows
    bf, f32 = jnp.bfloat16, jnp.float32
    dma = pltpu.SemaphoreType.DMA
    vmem = pl.BlockSpec(memory_space=pltpu.VMEM)
    hbm = pl.BlockSpec(memory_space=pl.ANY)
    scratch = [
        pltpu.VMEM((n_dev, rows, cols + (mix_w if j == 0 else 0)), bf) for j in range(CHUNKS)
    ] + [
        pltpu.VMEM((2 * exp_dev, width, ff), bf),
        pltpu.VMEM((exp_dev * ff, width), bf),
        pltpu.VMEM((2 * exp_dev, n_dev * rows, ff), f32),
        pltpu.VMEM((n_dev * rows, exp_dev * ff), bf),
        pltpu.VMEM((CHUNKS, half_rows, cols), bf),
        pltpu.VMEM((CHUNKS, half_rows, cols), bf),
        pltpu.VMEM((CHUNKS, half_rows, cols), f32),
        pltpu.VMEM((CHUNKS, col_rows, cols), bf),
        pltpu.VMEM((CHUNKS, col_rows, cols), bf),
        pltpu.VMEM((CHUNKS, nz, rows, cols), f32),
        pltpu.VMEM((CHUNKS, nz, rows, cols), bf),
        pltpu.VMEM((CHUNKS, nz, rows, cols), bf),
        pltpu.VMEM((CHUNKS, nz, rows, cols), bf),
        pltpu.VMEM((CHUNKS, nz, rows, cols), bf),
        dma((CHUNKS,)),
        dma((CHUNKS, 2 * exp_dev)),
        dma((exp_dev,)),
        dma((CHUNKS, 5, nz)),
        dma((CHUNKS, n_dev)),
        dma((CHUNKS,)),
        dma((CHUNKS,)),
        dma((CHUNKS,)),
        dma((CHUNKS,)),
        dma((CHUNKS, nz)),
        dma((CHUNKS, nz)),
        dma((CHUNKS, nz)),
        dma((CHUNKS, nz)),
    ]
    return pl.pallas_call(
        functools.partial(kernel, nz, experts),
        out_shape=jax.ShapeDtypeStruct((rows, width), bf),
        in_specs=[hbm, vmem, vmem, vmem, hbm, hbm, hbm],
        out_specs=vmem,
        scratch_shapes=scratch,
        compiler_params=pltpu.CompilerParams(
            collective_id=0, has_side_effects=True, vmem_limit_bytes=60 * 1024 * 1024
        ),
    )(tokens, expert_ids, combine_weights, plan, w_gate, w_up, w_down)


def local(tokens, expert_ids, combine_weights, slot_plan, w_gate, w_up, w_down):
    slots = slot_plan.shape[0]
    rows, top = expert_ids.shape
    capacity = max(2, (3 * rows * top + 2 * slots - 1) // (2 * slots))
    fits = 2 * capacity * w_gate.shape[0] >= rows
    body = dense_local if fits and lax.axis_size("rank") == 2 * CORES else sparse_local
    return body(tokens, expert_ids, combine_weights, slot_plan, w_gate, w_up, w_down)


def solution(mesh):
    in_specs = (
        P(("grp", "node", "rank"), None),
        P(("grp", "node", "rank"), None),
        P(("grp", "node", "rank"), None),
        P(),
        P(("node", "rank"), None, None),
        P(("node", "rank"), None, None),
        P(("node", "rank"), None, None),
    )
    out_specs = P(("grp", "node", "rank"), None)
    return jax.shard_map(local, mesh=mesh, in_specs=in_specs, out_specs=out_specs, check_vma=False)
```

```python
import functools
import jax
import jax.numpy as jnp
from jax import lax
from jax.experimental import pallas as pl
from jax.experimental.pallas import tpu as pltpu
from jax.sharding import PartitionSpec as P

CORES = 2
CHUNKS = 4
MESH = pl.DeviceIdType.MESH
CROSS, TWIN, RELAY, COLUMN = range(4)


def sparse_local(tokens, expert_ids, combine_weights, slot_plan, w_gate, w_up, w_down):
    n_node = lax.axis_size("node")
    n_rank = lax.axis_size("rank")
    n_dev = n_node * n_rank
    exp_dev = w_gate.shape[0]
    slots = n_dev * exp_dev
    tok_rows, top = expert_ids.shape
    width = tokens.shape[1]
    capacity = max(2, (3 * tok_rows * top + 2 * slots - 1) // (2 * slots))
    flat_ids = expert_ids.reshape(-1)
    onehot = (flat_ids[:, None] == jnp.arange(slots, dtype=jnp.int32)[None, :]).astype(jnp.int32)
    slot_of = jnp.sum(onehot * slot_plan[None, :], axis=1)
    earlier = jnp.cumsum(onehot, axis=0) - onehot
    position = jnp.sum(earlier * onehot, axis=1)
    target = slot_of * capacity + position
    repeated = jnp.repeat(tokens, top, axis=0)
    outgoing = jnp.zeros((slots * capacity, width), jnp.bfloat16).at[target].set(repeated)
    flat_out = outgoing.reshape(n_dev, exp_dev * capacity, width)
    arrived = lax.all_to_all(flat_out, ("node", "rank"), split_axis=0, concat_axis=0, tiled=True)
    arrived = arrived.reshape(n_dev, exp_dev, capacity, width)
    gate = jnp.einsum("secd,edf->secf", arrived, w_gate, preferred_element_type=jnp.float32)
    up = jnp.einsum("secd,edf->secf", arrived, w_up, preferred_element_type=jnp.float32)
    hidden = (jax.nn.silu(gate) * up).astype(jnp.bfloat16)
    result = jnp.einsum(
        "secf,efd->secd", hidden, w_down, preferred_element_type=jnp.float32
    ).astype(jnp.bfloat16)
    flat_back = result.reshape(n_dev, exp_dev * capacity, width)
    returned = lax.all_to_all(flat_back, ("node", "rank"), split_axis=0, concat_axis=0, tiled=True)
    returned = returned.reshape(slots * capacity, width)
    picked = returned[target].reshape(tok_rows, top, width)
    scales = combine_weights.astype(jnp.float32) / 65536.0
    mixed = jnp.sum(picked.astype(jnp.float32) * scales[:, :, None], axis=1)
    return mixed.astype(jnp.bfloat16)


def kernel(
    nz, experts, tok_hbm, ids_ref, wts_ref, plan_ref, wg_hbm, wu_hbm, wd_hbm, out_ref,
    *scratch,
):
    bufs = scratch[:CHUNKS]
    (wgu, wdn, acc, hid, s1, r1, k1, s2, r2, az, s3, r3,
     own_sem, wgu_sem, wd_sem, send_sem, recv_sem,
     s1_sem, r1_sem, s2_sem, r2_sem, s3_sem, r3_sem) = scratch[CHUNKS:]
    z = lax.axis_index("node")
    rank = lax.axis_index("rank")
    x, c = rank // CORES, rank % CORES
    rows, width = tok_hbm.shape
    cols = width // CHUNKS
    exp_dev, _, ff = wg_hbm.shape
    col_rows = nz * rows
    half = 2 * nz
    total_rows = 2 * half * rows
    mine = c * half + x * nz
    other = c * half + (1 - x) * nz
    across = {"rank": (1 - x) * CORES + c}
    twin = {"rank": x * CORES + (1 - c)}

    own = [
        pltpu.make_async_copy(
            tok_hbm.at[:, pl.ds(j * cols, cols)],
            bufs[j].at[mine + z, :, pl.ds(0, cols)],
            own_sem.at[j],
        )
        for j in range(CHUNKS)
    ]
    for copy in own:
        copy.start()

    barrier = pltpu.get_barrier_semaphore()

    def greet(device):
        pl.semaphore_signal(barrier, inc=1, device_id=device, device_id_type=MESH)

    greet(across)
    greet(twin)
    for d in range(1, nz):
        greet({"node": (z + d) % nz})

    gu_copies = []
    for j in range(CHUNKS):
        piece = []
        for e in range(exp_dev):
            for g, src in enumerate((wg_hbm, wu_hbm)):
                i = e * 2 + g
                piece.append(pltpu.make_async_copy(
                    src.at[e, pl.ds(j * cols, cols), :],
                    wgu.at[i, pl.ds(j * cols, cols), :],
                    wgu_sem.at[j, i],
                ))
        gu_copies.append(piece)
    d_copies = [
        pltpu.make_async_copy(wd_hbm.at[e], wdn.at[pl.ds(e * ff, ff), :], wd_sem.at[e])
        for e in range(exp_dev)
    ]
    for piece in gu_copies:
        for copy in piece:
            copy.start()
    for copy in d_copies:
        copy.start()

    mix_w = bufs[0].shape[2] - cols
    lane = lax.broadcasted_iota(jnp.int32, (rows, mix_w), 1)
    low = lane >= experts
    expert = jnp.where(low, lane - experts, lane)
    ids, wts = ids_ref[...], wts_ref[...]
    dense = jnp.zeros((rows, mix_w), jnp.int32)
    for k in range(ids.shape[1]):
        dense += jnp.where(ids[:, k:k + 1] == expert, wts[:, k:k + 1], 0)
    parts = jnp.where(low, dense & 255, dense >> 8)
    bufs[0][mine + z, :, cols:] = parts.astype(jnp.float32).astype(jnp.bfloat16)

    pl.semaphore_wait(barrier, nz + 1)

    def block_copy(j, slot, kind, row, device):
        return pltpu.make_async_remote_copy(
            src_ref=bufs[j].at[slot],
            dst_ref=bufs[j].at[slot],
            send_sem=send_sem.at[j, kind, row],
            recv_sem=recv_sem.at[j, slot],
            device_id=device,
            device_id_type=MESH,
        )

    def arrived(j, slot):
        block_copy(j, slot, RELAY, 0, twin).wait_recv()

    def spread(j, src):
        block_copy(j, mine + src, CROSS, src, across).start()
        block_copy(j, mine + src, TWIN, src, twin).start()

    def by_distance(dist, step):
        pl.when(z - dist >= 0)(lambda: step(z - dist))
        pl.when(z + dist <= nz - 1)(lambda: step(z + dist))

    def relay(j, src):
        arrived(j, other + src)
        block_copy(j, other + src, RELAY, src, twin).start()

    def to_column(j, dst):
        block_copy(j, mine + z, COLUMN + dst, 0, {"node": dst}).start()

    def from_column(j, src):
        arrived(j, mine + src)
        spread(j, src)

    def gather_step(j, step):
        if step == 0:
            own[j].wait()
            for dist in range(nz - 1, 0, -1):
                by_distance(dist, lambda t: to_column(j, t))
            spread(j, z)
        elif step == 1:
            relay(j, z)
            for dist in range(1, nz):
                by_distance(dist, lambda t: from_column(j, t))
        else:
            for dist in range(1, nz):
                by_distance(dist, lambda t: relay(j, t))

    def project(j):
        for s in range(half):
            arrived(j, (1 - c) * half + s)
        for copy in gu_copies[j]:
            copy.wait()

        def one(i, carry):
            block = bufs[j][:, :, :cols].reshape(total_rows, cols)
            part = jnp.dot(
                block, wgu[i, pl.ds(j * cols, cols), :], preferred_element_type=jnp.float32
            )
            if j == 0:
                acc[i] = part
            else:
                acc[i] = acc[i] + part
            return carry

        lax.fori_loop(0, 2 * exp_dev, one, 0)

    for wave in range(CHUNKS + 2):
        for step in range(3):
            j = wave - step
            if 0 <= j < CHUNKS:
                gather_step(j, step)
        if wave >= 2:
            project(wave - 2)

    device = z * lax.axis_size("rank") + rank
    mixes = bufs[0][:, :, cols:].reshape(total_rows, mix_w).astype(jnp.float32)
    lane_row = lax.broadcasted_iota(jnp.int32, (1, mix_w), 1)
    unit = jnp.where(lane_row < experts, 256.0 / 65536.0, 1.0 / 65536.0)
    for e in range(exp_dev):
        pick = jnp.where(plan_ref[...] == device * exp_dev + e, unit, 0.0)
        scale = jnp.sum(mixes * pick, axis=1, keepdims=True)
        gate = acc[2 * e]
        value = gate / (1.0 + jnp.exp(-gate)) * acc[2 * e + 1]
        hid[:, e * ff:(e + 1) * ff] = (value * scale).astype(jnp.bfloat16)
    for copy in d_copies:
        copy.wait()

    half_rows = half * rows

    def push(src, dst, ssem, rsem, dev):
        return pltpu.make_async_remote_copy(
            src_ref=src, dst_ref=dst, send_sem=ssem, recv_sem=rsem,
            device_id=dev, device_id_type=MESH,
        )

    def twin_copy(j):
        return push(s1.at[j], r1.at[j], s1_sem.at[j], r1_sem.at[j], twin)

    def cross_copy(j):
        return push(s2.at[j], r2.at[j], s2_sem.at[j], r2_sem.at[j], across)

    def column_copy(j, dst, src):
        return push(s3.at[j, dst], r3.at[j, src], s3_sem.at[j, dst], r3_sem.at[j, src], {"node": dst})

    def stage_down(j):
        w = wdn[:, j * cols:(j + 1) * cols]
        s1[j] = jnp.dot(
            hid[pl.ds((1 - c) * half_rows, half_rows), :], w, preferred_element_type=jnp.float32
        ).astype(jnp.bfloat16)
        twin_copy(j).start()
        k1[j] = jnp.dot(
            hid[pl.ds(c * half_rows, half_rows), :], w, preferred_element_type=jnp.float32
        )

    def stage_cross(j):
        twin_copy(j).wait_recv()
        away = pl.ds((1 - x) * col_rows, col_rows)
        s2[j] = (k1[j, away, :] + r1[j, away, :].astype(jnp.float32)).astype(jnp.bfloat16)
        cross_copy(j).start()

    def stage_column(j):
        cross_copy(j).wait_recv()
        near = pl.ds(x * col_rows, col_rows)
        total = k1[j, near, :] + r1[j, near, :].astype(jnp.float32) + r2[j].astype(jnp.float32)
        total = total.reshape(nz, rows, cols)
        az[j] = total
        s3[j] = total.astype(jnp.bfloat16)
        for dist in range(nz - 1, 0, -1):
            by_distance(dist, lambda t: column_copy(j, t, z).start())

    def stage_final(j):
        total = az[j, z]
        for d in range(1, nz):
            t = (z + d) % nz
            column_copy(j, z, t).wait_recv()
            total += r3[j, t].astype(jnp.float32)
        out_ref[:, j * cols:(j + 1) * cols] = total.astype(jnp.bfloat16)

    stages = (stage_down, stage_cross, stage_column, stage_final)
    for wave in range(CHUNKS + len(stages) - 1):
        for s, stage in enumerate(stages):
            if 0 <= wave - s < CHUNKS:
                stage(wave - s)

    for j in range(CHUNKS):
        for src in range(nz):
            block_copy(j, mine + src, CROSS, src, across).wait_send()
            block_copy(j, mine + src, TWIN, src, twin).wait_send()
            block_copy(j, other + src, RELAY, src, twin).wait_send()
        twin_copy(j).wait_send()
        cross_copy(j).wait_send()
        for d in range(1, nz):
            t = (z + d) % nz
            block_copy(j, mine + z, COLUMN + t, 0, {"node": t}).wait_send()
            column_copy(j, t, z).wait_send()


def dense_local(tokens, expert_ids, combine_weights, slot_plan, w_gate, w_up, w_down):
    nz = lax.axis_size("node")
    n_dev = nz * lax.axis_size("rank")
    rows, width = tokens.shape
    exp_dev, _, ff = w_gate.shape
    experts = slot_plan.shape[0]
    cols = width // CHUNKS
    mix_w = -(-2 * experts // 128) * 128
    plan = jnp.concatenate(
        [slot_plan, slot_plan, jnp.full((mix_w - 2 * experts,), -1, jnp.int32)]
    )[None, :]
    half = 2 * nz
    half_rows, col_rows = half * rows, nz * rows
    bf, f32 = jnp.bfloat16, jnp.float32
    dma = pltpu.SemaphoreType.DMA
    vmem = pl.BlockSpec(memory_space=pltpu.VMEM)
    hbm = pl.BlockSpec(memory_space=pl.ANY)
    scratch = [
        pltpu.VMEM((n_dev, rows, cols + (mix_w if j == 0 else 0)), bf) for j in range(CHUNKS)
    ] + [
        pltpu.VMEM((2 * exp_dev, width, ff), bf),
        pltpu.VMEM((exp_dev * ff, width), bf),
        pltpu.VMEM((2 * exp_dev, n_dev * rows, ff), f32),
        pltpu.VMEM((n_dev * rows, exp_dev * ff), bf),
        pltpu.VMEM((CHUNKS, half_rows, cols), bf),
        pltpu.VMEM((CHUNKS, half_rows, cols), bf),
        pltpu.VMEM((CHUNKS, half_rows, cols), f32),
        pltpu.VMEM((CHUNKS, col_rows, cols), bf),
        pltpu.VMEM((CHUNKS, col_rows, cols), bf),
        pltpu.VMEM((CHUNKS, nz, rows, cols), f32),
        pltpu.VMEM((CHUNKS, nz, rows, cols), bf),
        pltpu.VMEM((CHUNKS, nz, rows, cols), bf),
        dma((CHUNKS,)),
        dma((CHUNKS, 2 * exp_dev)),
        dma((exp_dev,)),
        dma((CHUNKS, 3 + nz, nz)),
        dma((CHUNKS, n_dev)),
        dma((CHUNKS,)),
        dma((CHUNKS,)),
        dma((CHUNKS,)),
        dma((CHUNKS,)),
        dma((CHUNKS, nz)),
        dma((CHUNKS, nz)),
    ]
    return pl.pallas_call(
        functools.partial(kernel, nz, experts),
        out_shape=jax.ShapeDtypeStruct((rows, width), bf),
        in_specs=[hbm, vmem, vmem, vmem, hbm, hbm, hbm],
        out_specs=vmem,
        scratch_shapes=scratch,
        compiler_params=pltpu.CompilerParams(
            collective_id=0, has_side_effects=True, vmem_limit_bytes=60 * 1024 * 1024
        ),
    )(tokens, expert_ids, combine_weights, plan, w_gate, w_up, w_down)


def local(tokens, expert_ids, combine_weights, slot_plan, w_gate, w_up, w_down):
    slots = slot_plan.shape[0]
    rows, top = expert_ids.shape
    capacity = max(2, (3 * rows * top + 2 * slots - 1) // (2 * slots))
    fits = 2 * capacity * w_gate.shape[0] >= rows
    body = dense_local if fits and lax.axis_size("rank") == 2 * CORES else sparse_local
    return body(tokens, expert_ids, combine_weights, slot_plan, w_gate, w_up, w_down)


def solution(mesh):
    in_specs = (
        P(("grp", "node", "rank"), None),
        P(("grp", "node", "rank"), None),
        P(("grp", "node", "rank"), None),
        P(),
        P(("node", "rank"), None, None),
        P(("node", "rank"), None, None),
        P(("node", "rank"), None, None),
    )
    out_specs = P(("grp", "node", "rank"), None)
    return jax.shard_map(local, mesh=mesh, in_specs=in_specs, out_specs=out_specs, check_vma=False)
```

```python
import functools
import jax
import jax.numpy as jnp
from jax import lax
from jax.experimental import pallas as pl
from jax.experimental.pallas import tpu as pltpu
from jax.sharding import PartitionSpec as P

CORES = 2
CHUNKS = 4
PIECES = 4
LAGS = (0, 1, 3, 5)
MESH = pl.DeviceIdType.MESH
CROSS, TWIN, RELAY, COLUMN = range(4)


def sparse_local(tokens, expert_ids, combine_weights, slot_plan, w_gate, w_up, w_down):
    n_node = lax.axis_size("node")
    n_rank = lax.axis_size("rank")
    n_dev = n_node * n_rank
    exp_dev = w_gate.shape[0]
    slots = n_dev * exp_dev
    tok_rows, top = expert_ids.shape
    width = tokens.shape[1]
    capacity = max(2, (3 * tok_rows * top + 2 * slots - 1) // (2 * slots))
    flat_ids = expert_ids.reshape(-1)
    onehot = (flat_ids[:, None] == jnp.arange(slots, dtype=jnp.int32)[None, :]).astype(jnp.int32)
    slot_of = jnp.sum(onehot * slot_plan[None, :], axis=1)
    earlier = jnp.cumsum(onehot, axis=0) - onehot
    position = jnp.sum(earlier * onehot, axis=1)
    target = slot_of * capacity + position
    repeated = jnp.repeat(tokens, top, axis=0)
    outgoing = jnp.zeros((slots * capacity, width), jnp.bfloat16).at[target].set(repeated)
    flat_out = outgoing.reshape(n_dev, exp_dev * capacity, width)
    arrived = lax.all_to_all(flat_out, ("node", "rank"), split_axis=0, concat_axis=0, tiled=True)
    arrived = arrived.reshape(n_dev, exp_dev, capacity, width)
    gate = jnp.einsum("secd,edf->secf", arrived, w_gate, preferred_element_type=jnp.float32)
    up = jnp.einsum("secd,edf->secf", arrived, w_up, preferred_element_type=jnp.float32)
    hidden = (jax.nn.silu(gate) * up).astype(jnp.bfloat16)
    result = jnp.einsum(
        "secf,efd->secd", hidden, w_down, preferred_element_type=jnp.float32
    ).astype(jnp.bfloat16)
    flat_back = result.reshape(n_dev, exp_dev * capacity, width)
    returned = lax.all_to_all(flat_back, ("node", "rank"), split_axis=0, concat_axis=0, tiled=True)
    returned = returned.reshape(slots * capacity, width)
    picked = returned[target].reshape(tok_rows, top, width)
    scales = combine_weights.astype(jnp.float32) / 65536.0
    mixed = jnp.sum(picked.astype(jnp.float32) * scales[:, :, None], axis=1)
    return mixed.astype(jnp.bfloat16)


def kernel(
    nz, experts, tok_hbm, ids_ref, wts_ref, plan_ref, wg_hbm, wu_hbm, wd_hbm, out_ref,
    *scratch,
):
    bufs = scratch[:CHUNKS]
    (wgu, wdn, acc, hid, s1, r1, k1, s2, r2, az, s3, r3,
     own_sem, wgu_sem, wd_sem, send_sem, recv_sem,
     s1_sem, r1_sem, s2_sem, r2_sem, s3_sem, r3_sem) = scratch[CHUNKS:]
    z = lax.axis_index("node")
    rank = lax.axis_index("rank")
    x, c = rank // CORES, rank % CORES
    rows, width = tok_hbm.shape
    cols = width // CHUNKS
    exp_dev, _, ff = wg_hbm.shape
    col_rows = nz * rows
    half = 2 * nz
    total_rows = 2 * half * rows
    mine = c * half + x * nz
    other = c * half + (1 - x) * nz
    across = {"rank": (1 - x) * CORES + c}
    twin = {"rank": x * CORES + (1 - c)}

    own = [
        pltpu.make_async_copy(
            tok_hbm.at[:, pl.ds(j * cols, cols)],
            bufs[j].at[mine + z, :, pl.ds(0, cols)],
            own_sem.at[j],
        )
        for j in range(CHUNKS)
    ]
    for copy in own:
        copy.start()

    barrier = pltpu.get_barrier_semaphore()

    def greet(device):
        pl.semaphore_signal(barrier, inc=1, device_id=device, device_id_type=MESH)

    greet(across)
    greet(twin)
    for d in range(1, nz):
        greet({"node": (z + d) % nz})

    gu_copies = []
    for j in range(CHUNKS):
        piece = []
        for e in range(exp_dev):
            for g, src in enumerate((wg_hbm, wu_hbm)):
                i = e * 2 + g
                piece.append(pltpu.make_async_copy(
                    src.at[e, pl.ds(j * cols, cols), :],
                    wgu.at[i, pl.ds(j * cols, cols), :],
                    wgu_sem.at[j, i],
                ))
        gu_copies.append(piece)
    d_copies = [
        pltpu.make_async_copy(wd_hbm.at[e], wdn.at[pl.ds(e * ff, ff), :], wd_sem.at[e])
        for e in range(exp_dev)
    ]
    for piece in gu_copies:
        for copy in piece:
            copy.start()
    for copy in d_copies:
        copy.start()

    mix_w = bufs[0].shape[2] - cols
    line = lax.broadcasted_iota(jnp.int32, (mix_w, rows), 0)
    low = line >= experts
    expert = jnp.where(low, line - experts, line)
    ids, wts = ids_ref[...], wts_ref[...]
    dense = jnp.zeros((mix_w, rows), jnp.int32)
    for k in range(ids.shape[0]):
        dense += jnp.where(ids[k:k + 1, :] == expert, wts[k:k + 1, :], 0)
    parts = jnp.where(low, dense & 255, dense >> 8).astype(jnp.float32).astype(jnp.bfloat16)
    eye = (
        lax.broadcasted_iota(jnp.int32, (rows, rows), 0)
        == lax.broadcasted_iota(jnp.int32, (rows, rows), 1)
    ).astype(jnp.float32).astype(jnp.bfloat16)
    turned = lax.dot_general(
        eye, parts, (((1,), (1,)), ((), ())), preferred_element_type=jnp.float32
    )
    bufs[0][mine + z, :, cols:] = turned.astype(jnp.bfloat16)

    pl.semaphore_wait(barrier, nz + 1)

    def block_copy(j, slot, kind, row, device):
        return pltpu.make_async_remote_copy(
            src_ref=bufs[j].at[slot],
            dst_ref=bufs[j].at[slot],
            send_sem=send_sem.at[j, kind, row],
            recv_sem=recv_sem.at[j, slot],
            device_id=device,
            device_id_type=MESH,
        )

    def arrived(j, slot):
        block_copy(j, slot, RELAY, 0, twin).wait_recv()

    def spread(j, src):
        block_copy(j, mine + src, CROSS, src, across).start()
        block_copy(j, mine + src, TWIN, src, twin).start()

    def by_distance(dist, step):
        pl.when(z - dist >= 0)(lambda: step(z - dist))
        pl.when(z + dist <= nz - 1)(lambda: step(z + dist))

    def relay(j, src):
        arrived(j, other + src)
        block_copy(j, other + src, RELAY, src, twin).start()

    def to_column(j, dst):
        block_copy(j, mine + z, COLUMN + dst, 0, {"node": dst}).start()

    def from_column(j, src):
        arrived(j, mine + src)
        spread(j, src)

    def pieces_of(j):
        steps = [lambda: relay(j, z)]
        for dist in range(1, nz):
            steps.append(lambda dist=dist: by_distance(dist, lambda t: from_column(j, t)))
        return steps

    def relays_of(j):
        return [
            lambda dist=dist: by_distance(dist, lambda t: relay(j, t)) for dist in range(1, nz)
        ]

    def dot_piece(j, i):
        block = bufs[j][:, :, :cols].reshape(total_rows, cols)
        part = jnp.dot(
            block, wgu[i, pl.ds(j * cols, cols), :], preferred_element_type=jnp.float32
        )
        acc[i] = part if j == 0 else acc[i] + part

    def ready(j):
        for s in range(half):
            arrived(j, (1 - c) * half + s)
        for copy in gu_copies[j]:
            copy.wait()

    for j in range(CHUNKS):
        own[j].wait()
        for dist in range(nz - 1, 0, -1):
            by_distance(dist, lambda t: to_column(j, t))
        spread(j, z)
    for wave in range(CHUNKS + 2):
        moves = []
        if wave < CHUNKS:
            moves += pieces_of(wave)
        if 1 <= wave <= CHUNKS:
            moves += relays_of(wave - 1)
        dots = []
        if wave >= 2:
            ready(wave - 2)
            dots = [lambda i=i: dot_piece(wave - 2, i) for i in range(2 * exp_dev)]
        for i in range(max(len(moves), len(dots))):
            if i < len(dots):
                dots[i]()
            if i < len(moves):
                moves[i]()

    device = z * lax.axis_size("rank") + rank
    mixes = bufs[0][:, :, cols:].reshape(total_rows, mix_w).astype(jnp.float32)
    high, small = mixes[:, :experts], mixes[:, experts:2 * experts]
    counts = high * (256.0 / 65536.0) + small * (1.0 / 65536.0)
    for e in range(exp_dev):
        pick = jnp.where(plan_ref[...] == device * exp_dev + e, 1.0, 0.0)
        scale = jnp.sum(counts * pick, axis=1, keepdims=True)
        gate = acc[2 * e]
        value = gate / (1.0 + jnp.exp(-gate)) * acc[2 * e + 1]
        hid[:, e * ff:(e + 1) * ff] = (value * scale).astype(jnp.bfloat16)
    for copy in d_copies:
        copy.wait()

    half_rows = half * rows
    span = width // PIECES

    def push(src, dst, ssem, rsem, dev):
        return pltpu.make_async_remote_copy(
            src_ref=src, dst_ref=dst, send_sem=ssem, recv_sem=rsem,
            device_id=dev, device_id_type=MESH,
        )

    def twin_copy(j):
        return push(s1.at[j], r1.at[j], s1_sem.at[j], r1_sem.at[j], twin)

    def cross_copy(j):
        return push(s2.at[j], r2.at[j], s2_sem.at[j], r2_sem.at[j], across)

    def column_copy(j, dst, src):
        return push(s3.at[j, dst], r3.at[j, src], s3_sem.at[j, dst], r3_sem.at[j, src], {"node": dst})

    def stage_down(j):
        w = wdn[:, j * span:(j + 1) * span]
        s1[j] = jnp.dot(
            hid[pl.ds((1 - c) * half_rows, half_rows), :], w, preferred_element_type=jnp.float32
        ).astype(jnp.bfloat16)
        twin_copy(j).start()
        k1[j] = jnp.dot(
            hid[pl.ds(c * half_rows, half_rows), :], w, preferred_element_type=jnp.float32
        )

    def stage_cross(j):
        twin_copy(j).wait_recv()
        away = pl.ds((1 - x) * col_rows, col_rows)
        s2[j] = (k1[j, away, :] + r1[j, away, :].astype(jnp.float32)).astype(jnp.bfloat16)
        cross_copy(j).start()

    def stage_column(j):
        cross_copy(j).wait_recv()
        near = pl.ds(x * col_rows, col_rows)
        total = k1[j, near, :] + r1[j, near, :].astype(jnp.float32) + r2[j].astype(jnp.float32)
        total = total.reshape(nz, rows, span)
        az[j] = total
        s3[j] = total.astype(jnp.bfloat16)
        for dist in range(nz - 1, 0, -1):
            by_distance(dist, lambda t: column_copy(j, t, z).start())

    def stage_final(j):
        total = az[j, z]
        for d in range(1, nz):
            t = (z + d) % nz
            column_copy(j, z, t).wait_recv()
            total += r3[j, t].astype(jnp.float32)
        out_ref[:, j * span:(j + 1) * span] = total.astype(jnp.bfloat16)

    stages = (stage_down, stage_cross, stage_column, stage_final)
    for wave in range(PIECES + LAGS[-1]):
        for lag, stage in zip(LAGS, stages):
            if 0 <= wave - lag < PIECES:
                stage(wave - lag)

    for j in range(CHUNKS):
        for src in range(nz):
            block_copy(j, mine + src, CROSS, src, across).wait_send()
            block_copy(j, mine + src, TWIN, src, twin).wait_send()
            block_copy(j, other + src, RELAY, src, twin).wait_send()
        for d in range(1, nz):
            t = (z + d) % nz
            block_copy(j, mine + z, COLUMN + t, 0, {"node": t}).wait_send()
    for j in range(PIECES):
        twin_copy(j).wait_send()
        cross_copy(j).wait_send()
        for d in range(1, nz):
            column_copy(j, (z + d) % nz, z).wait_send()


def dense_local(tokens, expert_ids, combine_weights, slot_plan, w_gate, w_up, w_down):
    nz = lax.axis_size("node")
    n_dev = nz * lax.axis_size("rank")
    rows, width = tokens.shape
    exp_dev, _, ff = w_gate.shape
    experts = slot_plan.shape[0]
    cols, span = width // CHUNKS, width // PIECES
    mix_w = -(-2 * experts // 128) * 128
    half = 2 * nz
    half_rows, col_rows = half * rows, nz * rows
    bf, f32 = jnp.bfloat16, jnp.float32
    dma = pltpu.SemaphoreType.DMA
    vmem = pl.BlockSpec(memory_space=pltpu.VMEM)
    hbm = pl.BlockSpec(memory_space=pl.ANY)
    scratch = [
        pltpu.VMEM((n_dev, rows, cols + (mix_w if j == 0 else 0)), bf) for j in range(CHUNKS)
    ] + [
        pltpu.VMEM((2 * exp_dev, width, ff), bf),
        pltpu.VMEM((exp_dev * ff, width), bf),
        pltpu.VMEM((2 * exp_dev, n_dev * rows, ff), f32),
        pltpu.VMEM((n_dev * rows, exp_dev * ff), bf),
        pltpu.VMEM((PIECES, half_rows, span), bf),
        pltpu.VMEM((PIECES, half_rows, span), bf),
        pltpu.VMEM((PIECES, half_rows, span), f32),
        pltpu.VMEM((PIECES, col_rows, span), bf),
        pltpu.VMEM((PIECES, col_rows, span), bf),
        pltpu.VMEM((PIECES, nz, rows, span), f32),
        pltpu.VMEM((PIECES, nz, rows, span), bf),
        pltpu.VMEM((PIECES, nz, rows, span), bf),
        dma((CHUNKS,)),
        dma((CHUNKS, 2 * exp_dev)),
        dma((exp_dev,)),
        dma((CHUNKS, 3 + nz, nz)),
        dma((CHUNKS, n_dev)),
        dma((PIECES,)),
        dma((PIECES,)),
        dma((PIECES,)),
        dma((PIECES,)),
        dma((PIECES, nz)),
        dma((PIECES, nz)),
    ]
    return pl.pallas_call(
        functools.partial(kernel, nz, experts),
        out_shape=jax.ShapeDtypeStruct((rows, width), bf),
        in_specs=[hbm, vmem, vmem, vmem, hbm, hbm, hbm],
        out_specs=vmem,
        scratch_shapes=scratch,
        compiler_params=pltpu.CompilerParams(
            collective_id=0, has_side_effects=True, vmem_limit_bytes=60 * 1024 * 1024
        ),
    )(tokens, expert_ids.T, combine_weights.T, slot_plan[None, :], w_gate, w_up, w_down)


def local(tokens, expert_ids, combine_weights, slot_plan, w_gate, w_up, w_down):
    slots = slot_plan.shape[0]
    rows, top = expert_ids.shape
    capacity = max(2, (3 * rows * top + 2 * slots - 1) // (2 * slots))
    fits = 2 * capacity * w_gate.shape[0] >= rows
    body = dense_local if fits and lax.axis_size("rank") == 2 * CORES else sparse_local
    return body(tokens, expert_ids, combine_weights, slot_plan, w_gate, w_up, w_down)


def solution(mesh):
    in_specs = (
        P(("grp", "node", "rank"), None),
        P(("grp", "node", "rank"), None),
        P(("grp", "node", "rank"), None),
        P(),
        P(("node", "rank"), None, None),
        P(("node", "rank"), None, None),
        P(("node", "rank"), None, None),
    )
    out_specs = P(("grp", "node", "rank"), None)
    return jax.shard_map(local, mesh=mesh, in_specs=in_specs, out_specs=out_specs, check_vma=False)
```

```python
import functools
import jax
import jax.numpy as jnp
from jax import lax
from jax.experimental import pallas as pl
from jax.experimental.pallas import tpu as pltpu
from jax.sharding import PartitionSpec as P

CORES = 2
CHUNKS = 2
PIECES = 4
LAGS = (0, 1, 3, 5)
MESH = pl.DeviceIdType.MESH
CROSS, TWIN, RELAY, COLUMN = range(4)


def sparse_local(tokens, expert_ids, combine_weights, slot_plan, w_gate, w_up, w_down):
    n_node = lax.axis_size("node")
    n_rank = lax.axis_size("rank")
    n_dev = n_node * n_rank
    exp_dev = w_gate.shape[0]
    slots = n_dev * exp_dev
    tok_rows, top = expert_ids.shape
    width = tokens.shape[1]
    capacity = max(2, (3 * tok_rows * top + 2 * slots - 1) // (2 * slots))
    flat_ids = expert_ids.reshape(-1)
    onehot = (flat_ids[:, None] == jnp.arange(slots, dtype=jnp.int32)[None, :]).astype(jnp.int32)
    slot_of = jnp.sum(onehot * slot_plan[None, :], axis=1)
    earlier = jnp.cumsum(onehot, axis=0) - onehot
    position = jnp.sum(earlier * onehot, axis=1)
    target = slot_of * capacity + position
    repeated = jnp.repeat(tokens, top, axis=0)
    outgoing = jnp.zeros((slots * capacity, width), jnp.bfloat16).at[target].set(repeated)
    flat_out = outgoing.reshape(n_dev, exp_dev * capacity, width)
    arrived = lax.all_to_all(flat_out, ("node", "rank"), split_axis=0, concat_axis=0, tiled=True)
    arrived = arrived.reshape(n_dev, exp_dev, capacity, width)
    gate = jnp.einsum("secd,edf->secf", arrived, w_gate, preferred_element_type=jnp.float32)
    up = jnp.einsum("secd,edf->secf", arrived, w_up, preferred_element_type=jnp.float32)
    hidden = (jax.nn.silu(gate) * up).astype(jnp.bfloat16)
    result = jnp.einsum(
        "secf,efd->secd", hidden, w_down, preferred_element_type=jnp.float32
    ).astype(jnp.bfloat16)
    flat_back = result.reshape(n_dev, exp_dev * capacity, width)
    returned = lax.all_to_all(flat_back, ("node", "rank"), split_axis=0, concat_axis=0, tiled=True)
    returned = returned.reshape(slots * capacity, width)
    picked = returned[target].reshape(tok_rows, top, width)
    scales = combine_weights.astype(jnp.float32) / 65536.0
    mixed = jnp.sum(picked.astype(jnp.float32) * scales[:, :, None], axis=1)
    return mixed.astype(jnp.bfloat16)


def kernel(
    nz, experts, tok_hbm, ids_ref, wts_ref, plan_ref, wg_hbm, wu_hbm, wd_hbm, out_ref,
    *scratch,
):
    bufs = scratch[:CHUNKS]
    (wgu, wdn, acc, hid, s1, r1, k1, s2, r2, az, s3, r3,
     own_sem, wgu_sem, wd_sem, send_sem, recv_sem,
     s1_sem, r1_sem, s2_sem, r2_sem, s3_sem, r3_sem) = scratch[CHUNKS:]
    z = lax.axis_index("node")
    rank = lax.axis_index("rank")
    x, c = rank // CORES, rank % CORES
    rows, width = tok_hbm.shape
    cols = width // CHUNKS
    exp_dev, _, ff = wg_hbm.shape
    col_rows = nz * rows
    half = 2 * nz
    total_rows = 2 * half * rows
    mine = c * half + x * nz
    other = c * half + (1 - x) * nz
    across = {"rank": (1 - x) * CORES + c}
    twin = {"rank": x * CORES + (1 - c)}

    own = [
        pltpu.make_async_copy(
            tok_hbm.at[:, pl.ds(j * cols, cols)],
            bufs[j].at[mine + z, :, pl.ds(0, cols)],
            own_sem.at[j],
        )
        for j in range(CHUNKS)
    ]
    for copy in own:
        copy.start()

    barrier = pltpu.get_barrier_semaphore()

    def greet(device):
        pl.semaphore_signal(barrier, inc=1, device_id=device, device_id_type=MESH)

    greet(across)
    greet(twin)
    for d in range(1, nz):
        greet({"node": (z + d) % nz})

    gu_copies = []
    for j in range(CHUNKS):
        piece = []
        for e in range(exp_dev):
            for g, src in enumerate((wg_hbm, wu_hbm)):
                i = e * 2 + g
                piece.append(pltpu.make_async_copy(
                    src.at[e, pl.ds(j * cols, cols), :],
                    wgu.at[i, pl.ds(j * cols, cols), :],
                    wgu_sem.at[j, i],
                ))
        gu_copies.append(piece)
    d_copies = [
        pltpu.make_async_copy(wd_hbm.at[e], wdn.at[pl.ds(e * ff, ff), :], wd_sem.at[e])
        for e in range(exp_dev)
    ]
    for piece in gu_copies:
        for copy in piece:
            copy.start()
    for copy in d_copies:
        copy.start()

    mix_w = bufs[0].shape[2] - cols
    line = lax.broadcasted_iota(jnp.int32, (mix_w, rows), 0)
    low = line >= experts
    expert = jnp.where(low, line - experts, line)
    ids, wts = ids_ref[...], wts_ref[...]
    dense = jnp.zeros((mix_w, rows), jnp.int32)
    for k in range(ids.shape[0]):
        dense += jnp.where(ids[k:k + 1, :] == expert, wts[k:k + 1, :], 0)
    parts = jnp.where(low, dense & 255, dense >> 8).astype(jnp.float32).astype(jnp.bfloat16)
    eye = (
        lax.broadcasted_iota(jnp.int32, (rows, rows), 0)
        == lax.broadcasted_iota(jnp.int32, (rows, rows), 1)
    ).astype(jnp.float32).astype(jnp.bfloat16)
    turned = lax.dot_general(
        eye, parts, (((1,), (1,)), ((), ())), preferred_element_type=jnp.float32
    )
    bufs[0][mine + z, :, cols:] = turned.astype(jnp.bfloat16)

    pl.semaphore_wait(barrier, nz + 1)

    def block_copy(j, slot, kind, row, device):
        return pltpu.make_async_remote_copy(
            src_ref=bufs[j].at[slot],
            dst_ref=bufs[j].at[slot],
            send_sem=send_sem.at[j, kind, row],
            recv_sem=recv_sem.at[j, slot],
            device_id=device,
            device_id_type=MESH,
        )

    def arrived(j, slot):
        block_copy(j, slot, RELAY, 0, twin).wait_recv()

    def spread(j, src):
        block_copy(j, mine + src, CROSS, src, across).start()
        block_copy(j, mine + src, TWIN, src, twin).start()

    def by_distance(dist, step):
        pl.when(z - dist >= 0)(lambda: step(z - dist))
        pl.when(z + dist <= nz - 1)(lambda: step(z + dist))

    def relay(j, src):
        arrived(j, other + src)
        block_copy(j, other + src, RELAY, src, twin).start()

    def upward(j, src):
        return block_copy(j, mine + src, COLUMN, src, {"node": z + 1})

    def downward(j, src):
        return block_copy(j, mine + src, COLUMN + 1, src, {"node": z - 1})

    def from_column(j, dist):
        @pl.when(z - dist >= 0)
        def _():
            arrived(j, mine + z - dist)
            pl.when(z < nz - 1)(lambda: upward(j, z - dist).start())
            spread(j, z - dist)

        @pl.when(z + dist <= nz - 1)
        def _():
            arrived(j, mine + z + dist)
            pl.when(z > 0)(lambda: downward(j, z + dist).start())
            spread(j, z + dist)

    def relays_of(j, dist):
        return [lambda: by_distance(dist, lambda t: relay(j, t))] if dist else [lambda: relay(j, z)]

    def dot_piece(j, i):
        block = bufs[j][:, :, :cols].reshape(total_rows, cols)
        part = jnp.dot(
            block, wgu[i, pl.ds(j * cols, cols), :], preferred_element_type=jnp.float32
        )
        acc[i] = part if j == 0 else acc[i] + part

    def ready(j):
        for s in range(half):
            arrived(j, (1 - c) * half + s)
        for copy in gu_copies[j]:
            copy.wait()

    for j in range(CHUNKS):
        own[j].wait()
        pl.when(z < nz - 1)(lambda: upward(j, z).start())
        pl.when(z > 0)(lambda: downward(j, z).start())
        spread(j, z)
    for wave in range(CHUNKS + nz):
        moves = []
        for dist in range(1, nz):
            j = wave - dist + 1
            if 0 <= j < CHUNKS:
                moves.append(lambda j=j, dist=dist: from_column(j, dist))
        for dist in range(nz):
            j = wave - dist
            if 0 <= j < CHUNKS:
                moves += relays_of(j, dist)
        dots = []
        if wave >= nz:
            ready(wave - nz)
            dots = [lambda i=i: dot_piece(wave - nz, i) for i in range(2 * exp_dev)]
        for i in range(max(len(moves), len(dots))):
            if i < len(dots):
                dots[i]()
            if i < len(moves):
                moves[i]()

    device = z * lax.axis_size("rank") + rank
    mixes = bufs[0][:, :, cols:].reshape(total_rows, mix_w).astype(jnp.float32)
    high, small = mixes[:, :experts], mixes[:, experts:2 * experts]
    counts = high * (256.0 / 65536.0) + small * (1.0 / 65536.0)
    for e in range(exp_dev):
        pick = jnp.where(plan_ref[...] == device * exp_dev + e, 1.0, 0.0)
        scale = jnp.sum(counts * pick, axis=1, keepdims=True)
        gate = acc[2 * e]
        value = gate / (1.0 + jnp.exp(-gate)) * acc[2 * e + 1]
        hid[:, e * ff:(e + 1) * ff] = (value * scale).astype(jnp.bfloat16)
    for copy in d_copies:
        copy.wait()

    half_rows = half * rows
    span = width // PIECES

    def push(src, dst, ssem, rsem, dev):
        return pltpu.make_async_remote_copy(
            src_ref=src, dst_ref=dst, send_sem=ssem, recv_sem=rsem,
            device_id=dev, device_id_type=MESH,
        )

    def twin_copy(j):
        return push(s1.at[j], r1.at[j], s1_sem.at[j], r1_sem.at[j], twin)

    def cross_copy(j):
        return push(s2.at[j], r2.at[j], s2_sem.at[j], r2_sem.at[j], across)

    def column_copy(j, dst, src):
        return push(s3.at[j, dst], r3.at[j, src], s3_sem.at[j, dst], r3_sem.at[j, src], {"node": dst})

    def stage_down(j):
        w = wdn[:, j * span:(j + 1) * span]
        s1[j] = jnp.dot(
            hid[pl.ds((1 - c) * half_rows, half_rows), :], w, preferred_element_type=jnp.float32
        ).astype(jnp.bfloat16)
        twin_copy(j).start()
        k1[j] = jnp.dot(
            hid[pl.ds(c * half_rows, half_rows), :], w, preferred_element_type=jnp.float32
        )

    def stage_cross(j):
        twin_copy(j).wait_recv()
        away = pl.ds((1 - x) * col_rows, col_rows)
        s2[j] = (k1[j, away, :] + r1[j, away, :].astype(jnp.float32)).astype(jnp.bfloat16)
        cross_copy(j).start()

    def stage_column(j):
        cross_copy(j).wait_recv()
        near = pl.ds(x * col_rows, col_rows)
        total = k1[j, near, :] + r1[j, near, :].astype(jnp.float32) + r2[j].astype(jnp.float32)
        total = total.reshape(nz, rows, span)
        az[j] = total
        s3[j] = total.astype(jnp.bfloat16)
        for dist in range(nz - 1, 0, -1):
            by_distance(dist, lambda t: column_copy(j, t, z).start())

    def stage_final(j):
        total = az[j, z]
        for d in range(1, nz):
            t = (z + d) % nz
            column_copy(j, z, t).wait_recv()
            total += r3[j, t].astype(jnp.float32)
        out_ref[:, j * span:(j + 1) * span] = total.astype(jnp.bfloat16)

    stages = (stage_down, stage_cross, stage_column, stage_final)
    for wave in range(PIECES + LAGS[-1]):
        for lag, stage in zip(LAGS, stages):
            if 0 <= wave - lag < PIECES:
                stage(wave - lag)

    for j in range(CHUNKS):
        for src in range(nz):
            block_copy(j, mine + src, CROSS, src, across).wait_send()
            block_copy(j, mine + src, TWIN, src, twin).wait_send()
            block_copy(j, other + src, RELAY, src, twin).wait_send()
        for src in range(nz):
            pl.when((z < nz - 1) & (src <= z))(lambda: upward(j, src).wait_send())
            pl.when((z > 0) & (src >= z))(lambda: downward(j, src).wait_send())
    for j in range(PIECES):
        twin_copy(j).wait_send()
        cross_copy(j).wait_send()
        for d in range(1, nz):
            column_copy(j, (z + d) % nz, z).wait_send()


def dense_local(tokens, expert_ids, combine_weights, slot_plan, w_gate, w_up, w_down):
    nz = lax.axis_size("node")
    n_dev = nz * lax.axis_size("rank")
    rows, width = tokens.shape
    exp_dev, _, ff = w_gate.shape
    experts = slot_plan.shape[0]
    cols, span = width // CHUNKS, width // PIECES
    mix_w = -(-2 * experts // 128) * 128
    half = 2 * nz
    half_rows, col_rows = half * rows, nz * rows
    bf, f32 = jnp.bfloat16, jnp.float32
    dma = pltpu.SemaphoreType.DMA
    vmem = pl.BlockSpec(memory_space=pltpu.VMEM)
    hbm = pl.BlockSpec(memory_space=pl.ANY)
    scratch = [
        pltpu.VMEM((n_dev, rows, cols + (mix_w if j == 0 else 0)), bf) for j in range(CHUNKS)
    ] + [
        pltpu.VMEM((2 * exp_dev, width, ff), bf),
        pltpu.VMEM((exp_dev * ff, width), bf),
        pltpu.VMEM((2 * exp_dev, n_dev * rows, ff), f32),
        pltpu.VMEM((n_dev * rows, exp_dev * ff), bf),
        pltpu.VMEM((PIECES, half_rows, span), bf),
        pltpu.VMEM((PIECES, half_rows, span), bf),
        pltpu.VMEM((PIECES, half_rows, span), f32),
        pltpu.VMEM((PIECES, col_rows, span), bf),
        pltpu.VMEM((PIECES, col_rows, span), bf),
        pltpu.VMEM((PIECES, nz, rows, span), f32),
        pltpu.VMEM((PIECES, nz, rows, span), bf),
        pltpu.VMEM((PIECES, nz, rows, span), bf),
        dma((CHUNKS,)),
        dma((CHUNKS, 2 * exp_dev)),
        dma((exp_dev,)),
        dma((CHUNKS, 3 + nz, nz)),
        dma((CHUNKS, n_dev)),
        dma((PIECES,)),
        dma((PIECES,)),
        dma((PIECES,)),
        dma((PIECES,)),
        dma((PIECES, nz)),
        dma((PIECES, nz)),
    ]
    return pl.pallas_call(
        functools.partial(kernel, nz, experts),
        out_shape=jax.ShapeDtypeStruct((rows, width), bf),
        in_specs=[hbm, vmem, vmem, vmem, hbm, hbm, hbm],
        out_specs=vmem,
        scratch_shapes=scratch,
        compiler_params=pltpu.CompilerParams(
            collective_id=0, has_side_effects=True, vmem_limit_bytes=60 * 1024 * 1024
        ),
    )(tokens, expert_ids.T, combine_weights.T, slot_plan[None, :], w_gate, w_up, w_down)


def local(tokens, expert_ids, combine_weights, slot_plan, w_gate, w_up, w_down):
    slots = slot_plan.shape[0]
    rows, top = expert_ids.shape
    capacity = max(2, (3 * rows * top + 2 * slots - 1) // (2 * slots))
    fits = 2 * capacity * w_gate.shape[0] >= rows
    body = dense_local if fits and lax.axis_size("rank") == 2 * CORES else sparse_local
    return body(tokens, expert_ids, combine_weights, slot_plan, w_gate, w_up, w_down)


def solution(mesh):
    in_specs = (
        P(("grp", "node", "rank"), None),
        P(("grp", "node", "rank"), None),
        P(("grp", "node", "rank"), None),
        P(),
        P(("node", "rank"), None, None),
        P(("node", "rank"), None, None),
        P(("node", "rank"), None, None),
    )
    out_specs = P(("grp", "node", "rank"), None)
    return jax.shard_map(local, mesh=mesh, in_specs=in_specs, out_specs=out_specs, check_vma=False)
```
